512 devices in a mesh: loop: 64 (over y_lo, z, core), grp: 8 (over x, y_hi).
Axes of the slice: x: 4, y: 4 (y_hi: 2, y_lo: 2; y = y_hi * 2 + y_lo), z: 16, core: 2. Of those that a mesh axis runs over, the one named last changes fastest.
Arguments:
- ratings: bfloat16 [2, 262144, 2048], P(None, ('loop', 'grp')), may hold values from -2.5 to 2.5, as said below
- user_factors: float32 [262144, 128], P(('loop', 'grp')), may hold values from -2 to 2
- user_accum: float32 [262144, 128], P(('loop', 'grp')), may hold values from 20 to 400
- item_factors: float32 [131072, 128], P('loop'), may hold values from -2 to 2
- item_accum: float32 [131072, 128], P('loop'), may hold values from 20 to 400
Outputs:
- users_out: float32 [262144, 128], P(('loop', 'grp'))
- items_out: float32 [131072, 128], P('loop')
The draws below stay inside these ranges and needn't reach their ends.
Inputs may be any that keep to these rules, and one draw needn't show every extreme that they name: `ratings`: each entry is 0 (unobserved) or has magnitude 0.5 or more.
All inputs are finite; a program needn't handle non-finite values.
Results may differ from the reference program's by a relative error of at most 0.0085.
Values may be sent and summed in bfloat16 or wider, within the bound.
A program may use at most 64 MiB of HBM per device.

```python
import math
import jax
import jax.numpy as jnp
from jax import lax

K = 128
UD = 512
IB = 2048
SUB = 2
INNER = 2
USERS = 262144
ITEMS = 131072
N_LOOP = 64
N_GRP = 8


def draw_ratings(key, part):
    keys = jax.random.split(jax.random.fold_in(key, 17), 5)
    row_log = jax.random.uniform(keys[0], (1, USERS, 1), minval=math.log(0.05), maxval=math.log(0.6))
    col_log = jax.random.uniform(keys[1], (1, 1, IB), minval=math.log(0.5), maxval=0.0)
    density = jnp.exp(row_log + col_log)
    keep = jax.random.uniform(keys[2], (SUB, USERS, IB)) < density
    magnitude = jax.random.uniform(keys[3], (SUB, USERS, IB), minval=0.5, maxval=2.5)
    positive = jax.random.uniform(keys[4], (SUB, USERS, IB)) < 0.5
    signed = jnp.where(positive, magnitude, -magnitude)
    return jnp.where(keep, signed, 0.0).astype(jnp.bfloat16)


def level_of(key, shape, cuts, low, largest):
    level = 1.0
    for axis_at, parts in cuts:
        heights = jax.random.uniform(jax.random.fold_in(jax.random.fold_in(key, 6), axis_at), (parts,), jnp.float32, low / len(cuts), largest / len(cuts))
        level = level * jnp.repeat(jnp.exp(heights), shape[axis_at] // parts).reshape((-1,) + (1,) * (len(shape) - 1 - axis_at))
    return level


def normal_values(rng, extent, spread, limit, shards=(), kind=jnp.bfloat16):
    values = jax.random.normal(rng, extent, jnp.float32) * spread
    if len(shards) > 0:
        values = level_of(rng, extent, shards, -0.22, 0.18) * values
    return jnp.clip(values, min=-limit, max=limit).astype(kind)


def setup_inputs(seed: int = 0) -> dict:
    streams_of = jax.random.split(jax.random.key(seed), 6)
    return {
        "ratings": draw_ratings(jax.random.fold_in(streams_of[5], 71), 0),
        "user_factors": normal_values(streams_of[1], (USERS, K), 0.3, 2.0, ((0, 512),), jnp.float32),
        "user_accum": jnp.clip(jnp.exp(math.log(400.0) - 2.9957323 * jax.random.uniform(streams_of[2], (USERS, K), jnp.float32) ** level_of(streams_of[2], (USERS, K), ((0, 512),), -0.2, 0.2)), 20.0, 400.0),
        "item_factors": normal_values(streams_of[3], (ITEMS, K), 0.3, 2.0, ((0, 64),), jnp.float32),
        "item_accum": jnp.clip(jnp.exp(math.log(400.0) - 2.9957323 * jax.random.uniform(streams_of[4], (ITEMS, K), jnp.float32) ** level_of(streams_of[4], (ITEMS, K), ((0, 64),), -0.2, 0.2)), 20.0, 400.0),
    }


shrink = 0.05
learn_rate = 0.2
tiny_eps = 1e-06

def worker_pass(operands):
    users, user_acc, items, item_acc, rates = operands
    rate_full = rates.astype(jnp.float32)
    observed = (jnp.abs(rate_full) > 0.25).astype(jnp.float32)
    for inner_step in range(INNER):
        user_half = users.astype(jnp.bfloat16)
        item_half = items.astype(jnp.bfloat16)
        predicted = jnp.dot(user_half, item_half.T, preferred_element_type=jnp.float32)
        resid = (observed * (rate_full - predicted)).astype(jnp.bfloat16)
        grad_user = -jnp.dot(resid, item_half, preferred_element_type=jnp.float32) + shrink * users
        terms = jnp.einsum('gui,guk->gik', resid.reshape(N_GRP, UD, IB).astype(jnp.float32), user_half.reshape(N_GRP, UD, K).astype(jnp.float32))
        rounded = lax.optimization_barrier((-terms).astype(jnp.bfloat16))
        grad_item = lax.optimization_barrier(jnp.sum(rounded.astype(jnp.float32), axis=0)) + shrink * items
        user_acc = user_acc + grad_user * grad_user
        users = users - learn_rate * grad_user / jnp.sqrt(user_acc + tiny_eps)
        item_acc = item_acc + grad_item * grad_item
        items = items - learn_rate * grad_item / jnp.sqrt(item_acc + tiny_eps)
    return (users, user_acc, items, item_acc)

def reference(ratings, user_factors, user_accum, item_factors, item_accum):
    users = user_factors.reshape(N_LOOP, N_GRP * UD, K)
    user_acc = user_accum.reshape(N_LOOP, N_GRP * UD, K)
    items = item_factors.reshape(N_LOOP, IB, K)
    item_acc = item_accum.reshape(N_LOOP, IB, K)
    rates = ratings.reshape(SUB, N_LOOP, N_GRP * UD, IB)
    for sub_epoch in range(SUB):
        if sub_epoch > 0:
            items = jnp.roll(items, 1, axis=0)
            item_acc = jnp.roll(item_acc, 1, axis=0)
        users, user_acc, items, item_acc = lax.map(worker_pass, (users, user_acc, items, item_acc, rates[sub_epoch]))
    return (users.reshape(USERS, K), items.reshape(ITEMS, K))
```

```python
import functools

import jax
import jax.numpy as jnp
from jax import lax
from jax.experimental import pallas as pl
from jax.experimental.pallas import tpu as pltpu
from jax.sharding import PartitionSpec as P

SUB = 2
INNER = 2
STEPS = SUB * INNER

shrink = 0.05
learn_rate = 0.2
tiny_eps = 1e-06

NC = 2
MESH = pl.DeviceIdType.MESH


def adagrad(param, accum, grad):
    accum = accum + grad * grad
    return param - learn_rate * grad / jnp.sqrt(accum + tiny_eps), accum


def kernel(
    n_loop, n_grp,
    ratings, user_in, uacc_in, item_in, iacc_in,
    users_out, items_out,
    rate, users, uacc, uhalf, gu, items0, vh, term, rs, vsh, bsh,
    load_sem, rs_send, rs_recv, ag_send, ag_recv, sh_send, sh_recv,
):
    me_l, me_g = lax.axis_index("loop"), lax.axis_index("grp")
    nxt, prv = lax.rem(me_l + 1, n_loop), lax.rem(me_l + n_loop - 1, n_loop)
    n_items = item_in.shape[0]
    span = n_items // NC
    piece = span // n_grp
    nb = span // 512
    per = n_grp // nb
    n_blocks = NC * nb

    barrier = pltpu.get_barrier_semaphore()

    def greet(k, _):
        other = lax.rem(me_g + k, n_grp)
        pl.semaphore_signal(barrier, inc=1, device_id=(nxt, other), device_id_type=MESH)
        pl.semaphore_signal(barrier, inc=1, device_id=(prv, other), device_id_type=MESH)

        @pl.when(k > 0)
        def _():
            pl.semaphore_signal(barrier, inc=1, device_id=(me_l, other), device_id_type=MESH)

        return 0

    lax.fori_loop(0, n_grp, greet, 0)

    def row_of(p, owner):
        return pl.multiple_of(p * span + owner * piece, piece)

    loads = [
        pltpu.make_async_copy(user_in, users, load_sem.at[0]),
        pltpu.make_async_copy(item_in, items0, load_sem.at[1]),
        pltpu.make_async_copy(ratings.at[0], rate.at[0], load_sem.at[2]),
        pltpu.make_async_copy(uacc_in, uacc, load_sem.at[3]),
    ]
    for p in range(NC):
        rows = pl.ds(row_of(p, me_g), piece)
        loads.append(pltpu.make_async_copy(iacc_in.at[rows], bsh.at[0, p], load_sem.at[4 + p]))
    loads.append(pltpu.make_async_copy(ratings.at[1], rate.at[1], load_sem.at[4 + NC]))
    for copy in loads:
        copy.start()
    loads[0].wait()
    loads[1].wait()
    uhalf[...] = users[...].astype(jnp.bfloat16)
    vh[0] = items0[...].astype(jnp.bfloat16)
    for p in range(NC):
        vsh[0, p] = items0[pl.ds(row_of(p, me_g), piece)]
    loads[2].wait()
    pl.semaphore_wait(barrier, 3 * n_grp - 1)

    def rs_copy(step, p, owner):
        rows = pl.ds(row_of(p, owner), piece)
        return pltpu.make_async_remote_copy(
            src_ref=term.at[step, rows],
            dst_ref=rs.at[step, p, me_g],
            send_sem=rs_send.at[step, p, owner],
            recv_sem=rs_recv.at[step, p, me_g],
            device_id=(me_l, owner),
            device_id_type=MESH,
        )

    def rs_wait(step, p, source):
        pltpu.make_async_remote_copy(
            src_ref=term.at[step, pl.ds(row_of(p, source), piece)],
            dst_ref=rs.at[step, p, source],
            send_sem=rs_send.at[step, p, source],
            recv_sem=rs_recv.at[step, p, source],
            device_id=(me_l, source),
            device_id_type=MESH,
        ).wait_recv()

    def ag_copy(step, p, worker, member):
        rows = pl.ds(row_of(p, me_g), piece)
        return pltpu.make_async_remote_copy(
            src_ref=vh.at[step + 1, rows],
            dst_ref=vh.at[step + 1, rows],
            send_sem=ag_send.at[step, p, member],
            recv_sem=ag_recv.at[step, p, me_g],
            device_id=(worker, member),
            device_id_type=MESH,
        )

    def ag_wait(step, p, source):
        rows = pl.ds(row_of(p, source), piece)
        pltpu.make_async_remote_copy(
            src_ref=vh.at[step + 1, rows],
            dst_ref=vh.at[step + 1, rows],
            send_sem=ag_send.at[step, p, source],
            recv_sem=ag_recv.at[step, p, source],
            device_id=(me_l, source),
            device_id_type=MESH,
        ).wait_recv()

    def shift_copies(p):
        return [
            pltpu.make_async_remote_copy(
                src_ref=ref.at[1, p],
                dst_ref=ref.at[2, p],
                send_sem=sh_send.at[i, p],
                recv_sem=sh_recv.at[i, p],
                device_id=(nxt, me_g),
                device_id_type=MESH,
            )
            for i, ref in enumerate((vsh, bsh))
        ]

    for step in range(STEPS):
        sub = step // INNER

        def block(j, _, step=step, sub=sub):
            p = j // nb
            b = lax.rem(j % nb + 1 + me_g // per, nb)
            first = pl.multiple_of(p * span + b * 512, 512)
            if step > 0:

                def arrive(q, _):
                    owner = b * per + q
                    if step == INNER:
                        ag_wait(step - 1, p, owner)
                    else:

                        @pl.when(owner != me_g)
                        def _():
                            ag_wait(step - 1, p, owner)

                    return 0

                lax.fori_loop(0, per, arrive, 0)
            user_half = uhalf[...]
            for t in range(2):
                rows = pl.ds(first + t * 256, 256)
                item_half = vh[step, rows]
                predicted = lax.dot_general(
                    user_half, item_half, (((1,), (1,)), ((), ())), preferred_element_type=jnp.float32
                )
                rate_full = rate[sub, :, rows].astype(jnp.float32)
                resid = jnp.where(jnp.abs(rate_full) > 0.25, rate_full - predicted, 0.0).astype(jnp.bfloat16)
                toward = jnp.dot(resid, item_half, preferred_element_type=jnp.float32)
                own = lax.dot_general(
                    resid, user_half, (((0,), (0,)), ((), ())), preferred_element_type=jnp.float32
                )
                term[step, rows] = (-own).astype(jnp.bfloat16)
                gu[...] += toward

            def give(q, _):
                owner = b * per + q

                @pl.when(owner != me_g)
                def _():
                    rs_copy(step, p, owner).start()

                return 0

            lax.fori_loop(0, per, give, 0)
            return 0

        gu[...] = jnp.zeros_like(gu)
        lax.fori_loop(0, n_blocks, block, 0)

        if step == 0:
            loads[3].wait()
            for p in range(NC):
                loads[4 + p].wait()
        if step == INNER - 1:
            loads[4 + NC].wait()
        grad_user = -gu[...] + shrink * users[...]
        new_users, new_acc = adagrad(users[...], uacc[...], grad_user)
        if step < STEPS - 1:
            users[...] = new_users
            uacc[...] = new_acc
            uhalf[...] = new_users.astype(jnp.bfloat16)
        else:
            users_out[...] = new_users

        if step == INNER:
            for p in range(NC):
                for copy in shift_copies(p):
                    copy.wait_recv()

        src, dst = {0: (0, 1), 1: (1, 1), 2: (2, 3), 3: (3, 3)}[step]

        def own_piece(p, _, step=step, src=src, dst=dst):
            rows = pl.ds(row_of(p, me_g), piece)

            def arrive(k, _):
                rs_wait(step, p, lax.rem(me_g + k, n_grp))
                return 0

            lax.fori_loop(1, n_grp, arrive, 0)
            rs[step, p, me_g] = term[step, rows]
            total = rs[step, p, 0].astype(jnp.float32)
            for k in range(1, n_grp):
                total += rs[step, p, k].astype(jnp.float32)
            items = vsh[src, p]
            grad_item = total + shrink * items
            new_items, new_acc = adagrad(items, bsh[src, p], grad_item)
            vsh[dst, p] = new_items
            bsh[dst, p] = new_acc
            if step == STEPS - 1:
                vh[step + 1, rows] = (new_items - vh[step, rows].astype(jnp.float32)).astype(jnp.bfloat16)
            elif step == INNER - 1:
                vh[STEPS + 1, rows] = new_items.astype(jnp.bfloat16)
            else:
                vh[step + 1, rows] = new_items.astype(jnp.bfloat16)

            if step == INNER - 1:

                def send_next(k, _):
                    member = lax.rem(me_g + k, n_grp)
                    pltpu.make_async_remote_copy(
                        src_ref=vh.at[STEPS + 1, rows],
                        dst_ref=vh.at[step + 1, rows],
                        send_sem=ag_send.at[step, p, member],
                        recv_sem=ag_recv.at[step, p, me_g],
                        device_id=(nxt, member),
                        device_id_type=MESH,
                    ).start()
                    return 0

                lax.fori_loop(0, n_grp, send_next, 0)
                for copy in shift_copies(p):
                    copy.start()
            else:

                def send(k, _):
                    ag_copy(step, p, me_l, lax.rem(me_g + k, n_grp)).start()
                    return 0

                lax.fori_loop(1, n_grp, send, 0)
            return 0

        lax.fori_loop(0, NC, own_piece, 0)

    def finish(p, _):
        def arrive(k, _):
            ag_wait(STEPS - 1, p, lax.rem(me_g + k, n_grp))
            return 0

        lax.fori_loop(1, n_grp, arrive, 0)
        rows = pl.ds(pl.multiple_of(p * span, span), span)
        items_out[rows] = vh[STEPS - 1, rows].astype(jnp.float32) + vh[STEPS, rows].astype(jnp.float32)
        return 0

    lax.fori_loop(0, NC, finish, 0)

    for step in range(STEPS):

        def drain(p, _, step=step):
            def one(k, _):
                member = lax.rem(me_g + k, n_grp)
                rs_copy(step, p, member).wait_send()
                ag_copy(step, p, me_l, member).wait_send()
                return 0

            lax.fori_loop(1, n_grp, one, 0)
            if step == INNER - 1:
                ag_copy(step, p, nxt, me_g).wait_send()
                for copy in shift_copies(p):
                    copy.wait_send()
            return 0

        lax.fori_loop(0, NC, drain, 0)


def local(n_loop, n_grp, ratings, user_factors, user_accum, item_factors, item_accum):
    n_users, rank = user_factors.shape
    n_items = item_factors.shape[0]
    piece = n_items // NC // n_grp
    f32, half = jnp.float32, jnp.bfloat16
    sems = pltpu.SemaphoreType.DMA
    return pl.pallas_call(
        functools.partial(kernel, n_loop, n_grp),
        out_shape=(
            jax.ShapeDtypeStruct((n_users, rank), f32),
            jax.ShapeDtypeStruct((n_items, rank), f32),
        ),
        in_specs=[pl.BlockSpec(memory_space=pl.ANY)] * 5,
        out_specs=[pl.BlockSpec(memory_space=pltpu.VMEM)] * 2,
        scratch_shapes=[
            pltpu.VMEM((SUB, n_users, n_items), half),
            pltpu.VMEM((n_users, rank), f32),
            pltpu.VMEM((n_users, rank), f32),
            pltpu.VMEM((n_users, rank), half),
            pltpu.VMEM((n_users, rank), f32),
            pltpu.VMEM((n_items, rank), f32),
            pltpu.VMEM((STEPS + 2, n_items, rank), half),
            pltpu.VMEM((STEPS, n_items, rank), half),
            pltpu.VMEM((STEPS, NC, n_grp, piece, rank), half),
            pltpu.VMEM((4, NC, piece, rank), f32),
            pltpu.VMEM((4, NC, piece, rank), f32),
            sems((5 + NC,)),
            sems((STEPS, NC, n_grp)),
            sems((STEPS, NC, n_grp)),
            sems((STEPS, NC, n_grp)),
            sems((STEPS, NC, n_grp)),
            sems((2, NC)),
            sems((2, NC)),
        ],
        compiler_params=pltpu.CompilerParams(collective_id=0, has_side_effects=True),
        name="epoch",
    )(ratings, user_factors, user_accum, item_factors, item_accum)


def solution(mesh):
    in_specs = (
        P(None, ("loop", "grp"), None),
        P(("loop", "grp"), None),
        P(("loop", "grp"), None),
        P("loop", None),
        P("loop", None),
    )
    out_specs = (P(("loop", "grp"), None), P("loop", None))
    body = functools.partial(local, mesh.shape["loop"], mesh.shape["grp"])
    return jax.shard_map(body, mesh=mesh, in_specs=in_specs, out_specs=out_specs, check_vma=False)
```

```python
import functools

import jax
import jax.numpy as jnp
from jax import lax
from jax.experimental import pallas as pl
from jax.experimental.pallas import tpu as pltpu
from jax.sharding import PartitionSpec as P

SUB = 2
INNER = 2
STEPS = SUB * INNER

shrink = 0.05
learn_rate = 0.2
tiny_eps = 1e-06

NC = 8
MESH = pl.DeviceIdType.MESH


def adagrad(param, accum, grad):
    accum = accum + grad * grad
    return param - learn_rate * grad / jnp.sqrt(accum + tiny_eps), accum


def kernel(
    n_loop, n_grp,
    ratings, user_in, uacc_in, item_in, iacc_in,
    users_out, items_out,
    rate, users, uacc, uhalf, gu, items0, vh, term, rs, vsh, bsh,
    load_sem, rs_send, rs_recv, ag_send, ag_recv, sh_send, sh_recv,
):
    me_l, me_g = lax.axis_index("loop"), lax.axis_index("grp")
    nxt, prv = lax.rem(me_l + 1, n_loop), lax.rem(me_l + n_loop - 1, n_loop)
    n_items = item_in.shape[0]
    span = n_items // NC
    piece = span // n_grp

    barrier = pltpu.get_barrier_semaphore()

    def greet(k, _):
        other = lax.rem(me_g + k, n_grp)
        pl.semaphore_signal(barrier, inc=1, device_id=(prv, other), device_id_type=MESH)

        @pl.when(k > 0)
        def _():
            pl.semaphore_signal(barrier, inc=1, device_id=(me_l, other), device_id_type=MESH)

        return 0

    lax.fori_loop(0, n_grp, greet, 0)

    def row_of(p, owner):
        return pl.multiple_of(p * span + owner * piece, piece)

    def load_items(p):
        rows = pl.ds(p * span, span)
        return pltpu.make_async_copy(item_in.at[rows], items0.at[rows], load_sem.at[4 + p])

    def load_rates(p):
        cols = pl.ds(p * span, span)
        return pltpu.make_async_copy(
            ratings.at[0, :, cols], rate.at[0, :, cols], load_sem.at[4 + NC + p]
        )

    def load_accum(p):
        rows = pl.ds(row_of(p, me_g), piece)
        return pltpu.make_async_copy(iacc_in.at[rows], bsh.at[0, p], load_sem.at[4 + 2 * NC + p])

    load_users = pltpu.make_async_copy(user_in, users, load_sem.at[0])
    load_uacc = pltpu.make_async_copy(uacc_in, uacc, load_sem.at[1])
    load_second = pltpu.make_async_copy(ratings.at[1], rate.at[1], load_sem.at[2])
    load_users.start()
    for p in range(NC):
        load_items(p).start()
        load_rates(p).start()
    load_uacc.start()
    for p in range(NC):
        load_accum(p).start()
    load_second.start()
    load_users.wait()
    uhalf[...] = users[...].astype(jnp.bfloat16)
    pl.semaphore_wait(barrier, 2 * n_grp - 1)

    def rs_copy(step, p, owner):
        return pltpu.make_async_remote_copy(
            src_ref=term.at[step, pl.ds(row_of(p, owner), piece)],
            dst_ref=rs.at[step, p, me_g],
            send_sem=rs_send.at[step],
            recv_sem=rs_recv.at[step, p],
            device_id=(me_l, owner),
            device_id_type=MESH,
        )

    def ag_copy(step, p, worker, member, outbox):
        rows = pl.ds(row_of(p, me_g), piece)
        return pltpu.make_async_remote_copy(
            src_ref=vh.at[outbox, rows],
            dst_ref=vh.at[step + 1, rows],
            send_sem=ag_send.at[step],
            recv_sem=ag_recv.at[step, p],
            device_id=(worker, member),
            device_id_type=MESH,
        )

    def await_rows(count, sem):
        rows = pl.ds(0, count)
        pltpu.make_async_copy(term.at[0, rows], term.at[0, rows], sem).wait()

    def shift_copies():
        return [
            pltpu.make_async_remote_copy(
                src_ref=ref.at[1],
                dst_ref=ref.at[2],
                send_sem=sh_send.at[i],
                recv_sem=sh_recv.at[i],
                device_id=(nxt, me_g),
                device_id_type=MESH,
            )
            for i, ref in enumerate((vsh, bsh))
        ]

    for step in range(STEPS):
        sub = step // INNER

        def block(j, _, step=step, sub=sub):
            p = j
            first = pl.multiple_of(p * span, span)
            if step == 0:
                rows = pl.ds(first, span)
                pltpu.make_async_copy(item_in.at[rows], items0.at[rows], load_sem.at[4 + p]).wait()
                pltpu.make_async_copy(
                    ratings.at[0, :, rows], rate.at[0, :, rows], load_sem.at[4 + NC + p]
                ).wait()
                vh[0, rows] = items0[rows].astype(jnp.bfloat16)
                vsh[0, p] = items0[pl.ds(row_of(p, me_g), piece)]
            else:
                senders = n_grp if step == INNER else n_grp - 1
                await_rows(senders * piece, ag_recv.at[step - 1, p])
            user_half = uhalf[...]
            for t in range(span // 256):
                rows = pl.ds(first + t * 256, 256)
                item_half = vh[step, rows]
                predicted = lax.dot_general(
                    user_half, item_half, (((1,), (1,)), ((), ())), preferred_element_type=jnp.float32
                )
                rate_full = rate[sub, :, rows].astype(jnp.float32)
                resid = jnp.where(jnp.abs(rate_full) > 0.25, rate_full - predicted, 0.0).astype(jnp.bfloat16)
                toward = jnp.dot(resid, item_half, preferred_element_type=jnp.float32)
                own = lax.dot_general(
                    resid, user_half, (((0,), (0,)), ((), ())), preferred_element_type=jnp.float32
                )
                term[step, rows] = (-own).astype(jnp.bfloat16)
                gu[...] += toward

            def give(k, _):
                rs_copy(step, p, lax.rem(me_g + k, n_grp)).start()
                return 0

            lax.fori_loop(1, n_grp, give, 0)
            return 0

        gu[...] = jnp.zeros_like(gu)
        lax.fori_loop(0, NC, block, 0)

        if step == 0:
            load_uacc.wait()
            for p in range(NC):
                load_accum(p).wait()
        if step == INNER - 1:
            load_second.wait()
        grad_user = -gu[...] + shrink * users[...]
        new_users, new_acc = adagrad(users[...], uacc[...], grad_user)
        if step < STEPS - 1:
            users[...] = new_users
            uacc[...] = new_acc
            uhalf[...] = new_users.astype(jnp.bfloat16)
        else:
            users_out[...] = new_users

        if step == INNER:
            for copy in shift_copies():
                copy.wait_recv()

        src, dst = {0: (0, 1), 1: (1, 1), 2: (2, 3), 3: (3, 3)}[step]

        def own_piece(p, _, step=step, src=src, dst=dst):
            rows = pl.ds(row_of(p, me_g), piece)

            await_rows((n_grp - 1) * piece, rs_recv.at[step, p])
            rs[step, p, me_g] = term[step, rows]
            total = rs[step, p, 0].astype(jnp.float32)
            for k in range(1, n_grp):
                total += rs[step, p, k].astype(jnp.float32)
            items = vsh[src, p]
            grad_item = total + shrink * items
            new_items, new_acc = adagrad(items, bsh[src, p], grad_item)
            vsh[dst, p] = new_items
            bsh[dst, p] = new_acc
            if step == STEPS - 1:
                vh[step + 1, rows] = (new_items - vh[step, rows].astype(jnp.float32)).astype(jnp.bfloat16)
            elif step == INNER - 1:
                vh[STEPS + 1, rows] = new_items.astype(jnp.bfloat16)
            else:
                vh[step + 1, rows] = new_items.astype(jnp.bfloat16)

            if step == INNER - 1:

                def send(k, _):
                    ag_copy(step, p, nxt, lax.rem(me_g + k, n_grp), STEPS + 1).start()
                    return 0

                lax.fori_loop(0, n_grp, send, 0)
            else:

                def send(k, _):
                    ag_copy(step, p, me_l, lax.rem(me_g + k, n_grp), step + 1).start()
                    return 0

                lax.fori_loop(1, n_grp, send, 0)
            return 0

        lax.fori_loop(0, NC, own_piece, 0)
        if step == INNER - 1:
            for copy in shift_copies():
                copy.start()

    def finish(p, _):
        await_rows((n_grp - 1) * piece, ag_recv.at[STEPS - 1, p])
        rows = pl.ds(pl.multiple_of(p * span, span), span)
        items_out[rows] = vh[STEPS - 1, rows].astype(jnp.float32) + vh[STEPS, rows].astype(jnp.float32)
        return 0

    lax.fori_loop(0, NC, finish, 0)

    for step in range(STEPS):
        await_rows((n_grp - 1) * piece * NC, rs_send.at[step])
        await_rows((n_grp if step == INNER - 1 else n_grp - 1) * piece * NC, ag_send.at[step])
    for copy in shift_copies():
        copy.wait_send()


def local(n_loop, n_grp, ratings, user_factors, user_accum, item_factors, item_accum):
    n_users, rank = user_factors.shape
    n_items = item_factors.shape[0]
    piece = n_items // NC // n_grp
    f32, half = jnp.float32, jnp.bfloat16
    sems = pltpu.SemaphoreType.DMA
    return pl.pallas_call(
        functools.partial(kernel, n_loop, n_grp),
        out_shape=(
            pltpu.VMEM((n_users, rank), f32),
            pltpu.VMEM((n_items, rank), f32),
        ),
        in_specs=[pl.BlockSpec(memory_space=pl.ANY)] * 5,
        out_specs=[pl.BlockSpec(memory_space=pltpu.VMEM)] * 2,
        scratch_shapes=[
            pltpu.VMEM((SUB, n_users, n_items), half),
            pltpu.VMEM((n_users, rank), f32),
            pltpu.VMEM((n_users, rank), f32),
            pltpu.VMEM((n_users, rank), half),
            pltpu.VMEM((n_users, rank), f32),
            pltpu.VMEM((n_items, rank), f32),
            pltpu.VMEM((STEPS + 2, n_items, rank), half),
            pltpu.VMEM((STEPS, n_items, rank), half),
            pltpu.VMEM((STEPS, NC, n_grp, piece, rank), half),
            pltpu.VMEM((4, NC, piece, rank), f32),
            pltpu.VMEM((4, NC, piece, rank), f32),
            sems((4 + 3 * NC,)),
            sems((STEPS,)),
            sems((STEPS, NC)),
            sems((STEPS,)),
            sems((STEPS, NC)),
            sems((2,)),
            sems((2,)),
        ],
        compiler_params=pltpu.CompilerParams(collective_id=0, has_side_effects=True),
        name="epoch",
    )(ratings, user_factors, user_accum, item_factors, item_accum)


def solution(mesh):
    in_specs = (
        P(None, ("loop", "grp"), None),
        P(("loop", "grp"), None),
        P(("loop", "grp"), None),
        P("loop", None),
        P("loop", None),
    )
    out_specs = (P(("loop", "grp"), None), P("loop", None))
    body = functools.partial(local, mesh.shape["loop"], mesh.shape["grp"])
    return jax.shard_map(body, mesh=mesh, in_specs=in_specs, out_specs=out_specs, check_vma=False)
```

```python
import functools

import jax
import jax.numpy as jnp
from jax import lax
from jax.experimental import pallas as pl
from jax.experimental.pallas import tpu as pltpu
from jax.sharding import PartitionSpec as P

SUB = 2
INNER = 2
STEPS = SUB * INNER

shrink = 0.05
learn_rate = 0.2
tiny_eps = 1e-06

NC = 8
AHEAD = NC // 2
MESH = pl.DeviceIdType.MESH

ORDER = ((2, 1), (2, 0), (1, 1), (3, 1), (1, 0), (3, 0), (0, 1), (0, 0))


def adagrad(param, accum, grad):
    accum = accum + grad * grad
    return param - learn_rate * grad / jnp.sqrt(accum + tiny_eps), accum


def kernel(
    n_loop, n_grp,
    ratings, user_in, uacc_in, item_in, iacc_in,
    users_out, items_out,
    rate, users, uacc, uhalf, gu, items0, vh, term, rs, vsh, bsh,
    load_sem, rs_send, rs_recv, ag_send, ag_recv, sh_send, sh_recv,
):
    me_l, me_g = lax.axis_index("loop"), lax.axis_index("grp")
    nxt, prv = lax.rem(me_l + 1, n_loop), lax.rem(me_l + n_loop - 1, n_loop)
    n_items = item_in.shape[0]
    span = n_items // NC
    piece = span // n_grp

    barrier = pltpu.get_barrier_semaphore()

    def greet(k, _):
        other = lax.rem(me_g + k, n_grp)
        pl.semaphore_signal(barrier, inc=1, device_id=(prv, other), device_id_type=MESH)

        @pl.when(k > 0)
        def _():
            pl.semaphore_signal(barrier, inc=1, device_id=(me_l, other), device_id_type=MESH)

        return 0

    lax.fori_loop(0, n_grp, greet, 0)

    def peer(k):
        dx, dy = ORDER[k]
        return lax.rem(me_g // 2 + dx, n_grp // 2) * 2 + lax.rem(me_g + dy, 2)

    def row_of(p, owner):
        return pl.multiple_of(p * span + owner * piece, piece)

    def load_items(p):
        rows = pl.ds(p * span, span)
        return pltpu.make_async_copy(item_in.at[rows], items0.at[rows], load_sem.at[4 + p])

    def load_rates(p):
        cols = pl.ds(p * span, span)
        return pltpu.make_async_copy(
            ratings.at[0, :, cols], rate.at[0, :, cols], load_sem.at[4 + NC + p]
        )

    def load_accum(p):
        rows = pl.ds(row_of(p, me_g), piece)
        return pltpu.make_async_copy(iacc_in.at[rows], bsh.at[0, p], load_sem.at[4 + 2 * NC + p])

    load_users = pltpu.make_async_copy(user_in, users, load_sem.at[0])
    load_uacc = pltpu.make_async_copy(uacc_in, uacc, load_sem.at[1])
    load_second = pltpu.make_async_copy(ratings.at[1], rate.at[1], load_sem.at[2])
    load_users.start()
    for p in range(NC):
        load_items(p).start()
        load_rates(p).start()
    load_uacc.start()
    for p in range(NC):
        load_accum(p).start()
    load_second.start()
    gu[...] = jnp.zeros_like(gu)
    load_users.wait()
    uhalf[...] = users[...].astype(jnp.bfloat16)
    pl.semaphore_wait(barrier, 2 * n_grp - 1)

    def rs_copy(step, p, owner):
        return pltpu.make_async_remote_copy(
            src_ref=term.at[step, pl.ds(row_of(p, owner), piece)],
            dst_ref=rs.at[step, p, me_g],
            send_sem=rs_send.at[step],
            recv_sem=rs_recv.at[step, p],
            device_id=(me_l, owner),
            device_id_type=MESH,
        )

    def ag_copy(step, p, worker, member, outbox):
        rows = pl.ds(row_of(p, me_g), piece)
        return pltpu.make_async_remote_copy(
            src_ref=vh.at[outbox, rows],
            dst_ref=vh.at[step + 1, rows],
            send_sem=ag_send.at[step],
            recv_sem=ag_recv.at[step, p],
            device_id=(worker, member),
            device_id_type=MESH,
        )

    def await_rows(count, sem):
        rows = pl.ds(0, count)
        pltpu.make_async_copy(term.at[0, rows], term.at[0, rows], sem).wait()

    def shift_copies():
        return [
            pltpu.make_async_remote_copy(
                src_ref=ref.at[1],
                dst_ref=ref.at[2],
                send_sem=sh_send.at[i],
                recv_sem=sh_recv.at[i],
                device_id=(nxt, me_g),
                device_id_type=MESH,
            )
            for i, ref in enumerate((vsh, bsh))
        ]

    for step in range(STEPS):
        sub = step // INNER

        def block(j, _, step=step, sub=sub):
            p = j
            first = pl.multiple_of(p * span, span)
            if step == 0:
                rows = pl.ds(first, span)
                pltpu.make_async_copy(item_in.at[rows], items0.at[rows], load_sem.at[4 + p]).wait()
                pltpu.make_async_copy(
                    ratings.at[0, :, rows], rate.at[0, :, rows], load_sem.at[4 + NC + p]
                ).wait()
                vh[0, rows] = items0[rows].astype(jnp.bfloat16)
                vsh[0, p] = items0[pl.ds(row_of(p, me_g), piece)]
            else:
                senders = n_grp if step == INNER else n_grp - 1
                await_rows(senders * piece, ag_recv.at[step - 1, p])
            user_half = uhalf[...]
            for t in range(span // 256):
                rows = pl.ds(first + t * 256, 256)
                item_half = vh[step, rows]
                predicted = lax.dot_general(
                    user_half, item_half, (((1,), (1,)), ((), ())), preferred_element_type=jnp.float32
                )
                rate_full = rate[sub, :, rows].astype(jnp.float32)
                resid = jnp.where(jnp.abs(rate_full) > 0.25, rate_full - predicted, 0.0).astype(jnp.bfloat16)
                toward = jnp.dot(resid, item_half, preferred_element_type=jnp.float32)
                own = lax.dot_general(
                    resid, user_half, (((0,), (0,)), ((), ())), preferred_element_type=jnp.float32
                )
                term[step, rows] = (-own).astype(jnp.bfloat16)
                gu[...] += toward

            for k in range(n_grp - 1):
                rs_copy(step, p, peer(k)).start()
            return 0

        lax.fori_loop(0, NC, block, 0)

        if step == 0:
            load_uacc.wait()
            for p in range(NC):
                load_accum(p).wait()
        if step == INNER - 1:
            load_second.wait()
        def user_step(step=step):
            grad_user = -gu[...] + shrink * users[...]
            new_users, new_acc = adagrad(users[...], uacc[...], grad_user)
            if step < STEPS - 1:
                users[...] = new_users
                uacc[...] = new_acc
                uhalf[...] = new_users.astype(jnp.bfloat16)
                gu[...] = jnp.zeros_like(gu)
            else:
                users_out[...] = new_users

        if step == INNER:
            for copy in shift_copies():
                copy.wait_recv()

        src, dst = {0: (0, 1), 1: (1, 1), 2: (2, 3), 3: (3, 3)}[step]

        def own_piece(p, _, step=step, src=src, dst=dst):
            rows = pl.ds(row_of(p, me_g), piece)

            await_rows((n_grp - 1) * piece, rs_recv.at[step, p])
            rs[step, p, me_g] = term[step, rows]
            total = rs[step, p, 0].astype(jnp.float32)
            for k in range(1, n_grp):
                total += rs[step, p, k].astype(jnp.float32)
            items = vsh[src, p]
            grad_item = total + shrink * items
            new_items, new_acc = adagrad(items, bsh[src, p], grad_item)
            vsh[dst, p] = new_items
            bsh[dst, p] = new_acc
            if step == STEPS - 1:
                vh[step + 1, rows] = (new_items - vh[step, rows].astype(jnp.float32)).astype(jnp.bfloat16)
            elif step == INNER - 1:
                vh[STEPS + 1, rows] = new_items.astype(jnp.bfloat16)
            else:
                vh[step + 1, rows] = new_items.astype(jnp.bfloat16)

            if step == INNER - 1:
                for k in range(n_grp):
                    ag_copy(step, p, nxt, peer(k), STEPS + 1).start()
            else:
                for k in range(n_grp - 1):
                    ag_copy(step, p, me_l, peer(k), step + 1).start()
            return 0

        lax.fori_loop(0, AHEAD, own_piece, 0)
        user_step()
        lax.fori_loop(AHEAD, NC, own_piece, 0)
        if step == INNER - 1:
            for copy in shift_copies():
                copy.start()

    def finish(p, _):
        await_rows((n_grp - 1) * piece, ag_recv.at[STEPS - 1, p])
        rows = pl.ds(pl.multiple_of(p * span, span), span)
        items_out[rows] = vh[STEPS - 1, rows].astype(jnp.float32) + vh[STEPS, rows].astype(jnp.float32)
        return 0

    lax.fori_loop(0, NC, finish, 0)

    for step in range(STEPS):
        await_rows((n_grp - 1) * piece * NC, rs_send.at[step])
        await_rows((n_grp if step == INNER - 1 else n_grp - 1) * piece * NC, ag_send.at[step])
    for copy in shift_copies():
        copy.wait_send()


def publish(users, items, users_out, items_out, sem):
    copies = [
        pltpu.make_async_copy(items, items_out, sem.at[0]),
        pltpu.make_async_copy(users, users_out, sem.at[1]),
    ]
    for copy in copies:
        copy.start()
    for copy in copies:
        copy.wait()


def local(n_loop, n_grp, ratings, user_factors, user_accum, item_factors, item_accum):
    n_users, rank = user_factors.shape
    n_items = item_factors.shape[0]
    piece = n_items // NC // n_grp
    f32, half = jnp.float32, jnp.bfloat16
    sems = pltpu.SemaphoreType.DMA
    users, items = pl.pallas_call(
        functools.partial(kernel, n_loop, n_grp),
        out_shape=(
            pltpu.VMEM((n_users, rank), f32),
            pltpu.VMEM((n_items, rank), f32),
        ),
        in_specs=[pl.BlockSpec(memory_space=pl.ANY)] * 5,
        out_specs=[pl.BlockSpec(memory_space=pltpu.VMEM)] * 2,
        scratch_shapes=[
            pltpu.VMEM((SUB, n_users, n_items), half),
            pltpu.VMEM((n_users, rank), f32),
            pltpu.VMEM((n_users, rank), f32),
            pltpu.VMEM((n_users, rank), half),
            pltpu.VMEM((n_users, rank), f32),
            pltpu.VMEM((n_items, rank), f32),
            pltpu.VMEM((STEPS + 2, n_items, rank), half),
            pltpu.VMEM((STEPS, n_items, rank), half),
            pltpu.VMEM((STEPS, NC, n_grp, piece, rank), half),
            pltpu.VMEM((4, NC, piece, rank), f32),
            pltpu.VMEM((4, NC, piece, rank), f32),
            sems((4 + 3 * NC,)),
            sems((STEPS,)),
            sems((STEPS, NC)),
            sems((STEPS,)),
            sems((STEPS, NC)),
            sems((2,)),
            sems((2,)),
        ],
        compiler_params=pltpu.CompilerParams(collective_id=0, has_side_effects=True),
        name="epoch",
    )(ratings, user_factors, user_accum, item_factors, item_accum)
    return pl.pallas_call(
        publish,
        out_shape=(
            jax.ShapeDtypeStruct((n_users, rank), f32),
            jax.ShapeDtypeStruct((n_items, rank), f32),
        ),
        in_specs=[pl.BlockSpec(memory_space=pltpu.VMEM)] * 2,
        out_specs=[pl.BlockSpec(memory_space=pl.ANY)] * 2,
        scratch_shapes=[sems((2,))],
        name="publish",
    )(pltpu.with_memory_space_constraint(users, pltpu.VMEM), pltpu.with_memory_space_constraint(items, pltpu.VMEM))


def solution(mesh):
    in_specs = (
        P(None, ("loop", "grp"), None),
        P(("loop", "grp"), None),
        P(("loop", "grp"), None),
        P("loop", None),
        P("loop", None),
    )
    out_specs = (P(("loop", "grp"), None), P("loop", None))
    body = functools.partial(local, mesh.shape["loop"], mesh.shape["grp"])
    return jax.shard_map(body, mesh=mesh, in_specs=in_specs, out_specs=out_specs, check_vma=False)
```
